256 devices in a mesh: row: 16 (over z_hi, x), col: 16 (over z_lo, y, core).
Axes of the slice: x: 4, y: 4, z: 8 (z_hi: 4, z_lo: 2; z = z_hi * 2 + z_lo), core: 2. Of those that a mesh axis runs over, the one named last changes fastest.
Arguments:
- amplitudes: bfloat16 [64, 64, 768], P('row', None, 'col'), may hold values from -6 to 6
- integrals: bfloat16 [768, 384, 384], P('row', 'col'), may hold values from -0.21875 to 0.21875
Outputs:
- ladder: bfloat16 [64, 64, 384, 384], P('row', None, 'col')
The draws below stay inside these ranges and needn't reach their ends.
All inputs are finite; a program needn't handle non-finite values.
Results may differ from the reference program's by a relative error of at most 0.009.
Values may be sent and summed in bfloat16 or wider, within the bound.
No kernel may reach another device: no remote copies, remote signals or barrier semaphores. Data moves between devices by JAX's collectives and lax.ppermute only.
A program may use at most 128 MiB of HBM per device.

```python
import jax
import jax.numpy as jnp
from jax import lax

O = 64
VW = 384
CDT = 768


def shard_levels(own_key, extent, shards, low, top_value):
    level, own = 1.0, jax.random.fold_in(own_key, 6)
    for axis_at, shards_of in shards:
        draws = jnp.exp(jax.random.uniform(jax.random.fold_in(own, axis_at), (shards_of,), jnp.float32, low / len(shards), top_value / len(shards)))
        level = level * jnp.repeat(draws, extent[axis_at] // shards_of).reshape([-1 if axis == axis_at else 1 for axis in range(len(extent))])
    return level


def gaussian(key, shape, deviation, limit, shards=(), kind=jnp.bfloat16):
    array = jax.random.normal(key, shape, jnp.float32) * deviation
    if len(shards) > 0:
        array = shard_levels(key, shape, shards, -0.22, 0.18) * array
    return jnp.clip(array, min=-limit, max=limit).astype(kind)


def setup_inputs(seed: int = 0) -> dict:
    key_list = jax.random.split(jax.random.key(seed), 3)
    return {
        "amplitudes": gaussian(key_list[0], (O, O, CDT), 1.0, 6.0, ((0, 16), (2, 16))),
        "integrals": gaussian(key_list[1], (CDT, VW, VW), CDT ** -0.5, 0.21875, ((0, 16), (1, 16))),
    }


def reference(amplitudes, integrals):
    flat = integrals.reshape(CDT, VW * VW)

    def one_row(index):
        direct = jnp.dot(amplitudes[index], flat, preferred_element_type=jnp.float32).astype(jnp.bfloat16)
        column = lax.dynamic_index_in_dim(amplitudes, index, 1, keepdims=False)
        mirror = jnp.dot(column, flat, preferred_element_type=jnp.float32).astype(jnp.bfloat16)
        mirror = mirror.reshape(O, VW, VW).transpose(0, 2, 1)
        total = direct.reshape(O, VW, VW).astype(jnp.float32) + mirror.astype(jnp.float32)
        return total.astype(jnp.bfloat16)

    return lax.map(one_row, jnp.arange(O, dtype=jnp.int32))
```

```python
import jax
import jax.numpy as jnp
import numpy as np
from jax import lax
from jax.sharding import Mesh, PartitionSpec as P

AXES = ("zh", "x", "zl", "y", "core")
SIZES = (4, 4, 2, 4, 2)
BF = jnp.bfloat16
F32 = jnp.float32
CHUNKS = (((0, 0), (0, 1), (1, 0)), ((1, 1), (0, 2), (2, 0)), ((2, 2), (1, 2), (2, 1)))


def pairs(move):
    out = []
    for i in range(256):
        here = dict(zip(AXES, (int(v) for v in np.unravel_index(i, SIZES))))
        there = move(dict(here))
        out.append((i, int(np.ravel_multi_index([there[a] for a in AXES], SIZES))))
    return out


def along_z(step):
    def move(d):
        z = (d["zh"] * 2 + d["zl"] + step) % 8
        d["zh"], d["zl"] = z // 2, z % 2
        return d

    return pairs(move)


def along(axis, step):
    size = SIZES[AXES.index(axis)]

    def move(d):
        d[axis] = (d[axis] + step) % size
        return d

    return pairs(move)


def mirror(d):
    d["y"] = (d["x"] - d["y"]) % 4
    return d


def send(value, table):
    return lax.ppermute(value, AXES, table)


def one_hot(source, rows):
    at = lax.broadcasted_iota(jnp.int32, (rows, source.shape[0]), 0)
    return (at == source[None, :]).astype(BF)


def digits(sizes):
    n = int(np.prod(sizes))
    return [jnp.asarray(v, jnp.int32) for v in np.unravel_index(np.arange(n), sizes)]


def dot(a, b):
    return jnp.dot(a, b, preferred_element_type=F32)


def per_device(amplitudes, integrals):
    oi, oj, kk = amplitudes.shape
    va, vb = integrals.shape[1:]
    u = va // 3
    t = 2 * u * u
    rows = oi * oj
    zh, x, zl, y, core = (lax.axis_index(a) for a in AXES)

    dx, s2, a8, cb, b8 = digits((4, 3, u, 2, u))
    yb = (dx - y) % 4
    source = (((a8 * 4 + yb) * 2 + cb) * 3 + s2) * u + b8
    spread = one_hot(source, 12 * t)
    v = integrals.reshape(kk, 3, u, 2, vb // 2)
    v = jnp.transpose(v, (3, 1, 0, 2, 4)).reshape(6 * kk, u * vb // 2)
    v = dot(v, spread).astype(BF)
    v = v.reshape(2, 3, kk, 4, 3, t)
    v = jnp.transpose(v, (3, 0, 1, 4, 2, 5))
    v = lax.all_to_all(v.reshape(4, -1, t), "x", 0, 0, tiled=True)
    v = v.reshape(4, 2, 3, 3, kk, t)

    direct = jnp.transpose(amplitudes, (2, 0, 1)).reshape(kk, rows)
    turned = amplitudes.reshape(oi, 4, 4 * oi, kk)
    turned = lax.all_to_all(jnp.transpose(turned, (1, 3, 0, 2)), "zh", 0, 0, tiled=True)
    turned = jnp.transpose(turned, (1, 0, 2, 3)).reshape(kk, rows)
    amp = jnp.concatenate([direct, turned], axis=1)
    amp = jnp.broadcast_to(amp[None], (16, kk, 2 * rows))
    amp = lax.all_to_all(amp, ("zl", "y", "core"), 0, 0, tiled=True)
    from_x = [amp] + [send(amp, along("x", -d)) for d in (1, 2, 3)]
    amp = jnp.stack(from_x)
    amp = jnp.roll(amp.reshape(4, 4, 4 * kk, 2 * rows), -zh, axis=1)
    direct = amp[..., :rows].reshape(4, 16 * kk, rows)
    direct = jnp.transpose(direct, (0, 2, 1)).reshape(4 * rows, 16 * kk)
    turned = amp[..., rows:].reshape(4, 16 * kk, 4, oi, 4, oi)
    turned = jnp.roll(jnp.roll(turned, x, axis=0), -x, axis=4)
    turned = jnp.transpose(turned, (4, 5, 2, 0, 3, 1)).reshape(4 * rows, 16 * kk)
    turned_odd = turned.reshape(4 * rows, 4, 4 * kk)
    turned_odd = jnp.roll(turned_odd, -zl, axis=1).reshape(4 * rows, 16 * kk)
    left = (
        jnp.concatenate([direct, turned], axis=1),
        jnp.concatenate([direct, turned_odd], axis=1),
    )

    a8, cb, b8 = digits((u, 2, u))
    place = (b8 * 2 + core) * u + a8
    keep_own = one_hot(jnp.where(cb == core, place, -1), t)
    keep_other = one_hot(jnp.where(cb != core, place, -1), t)

    results = {}
    for blocks in CHUNKS:
        nb = len(blocks)
        slab = jnp.stack([v[:, :, s, q] for s, q in blocks], axis=2)
        slab = jnp.transpose(slab, (1, 2, 0, 3, 4)).reshape(2, nb, 4 * kk, t)
        slabs = {0: slab}
        up = down = slab
        for step in (1, 2, 3):
            up, down = send(up, along_z(1)), send(down, along_z(-1))
            slabs[8 - step], slabs[step] = up, down
        slabs[4] = jnp.stack([send(up[0], along_z(1)), send(down[1], along_z(-1))])
        got = {}
        for group in ((0, 1, 7), (2, 6), (3, 5), (4,)):
            part = jnp.stack([lax.dynamic_index_in_dim(slabs[g], zl, 0, False) for g in group])
            part = send(part, pairs(mirror))
            other = send(part, along("core", 1))
            for n, g in enumerate(group):
                turn = [blocks.index((q, s)) for s, q in blocks]
                own_g = jnp.stack([part[n, i] for i in turn]).reshape(-1, t)
                other_g = jnp.stack([other[n, i] for i in turn]).reshape(-1, t)
                both = dot(own_g, keep_own) + dot(other_g, keep_other)
                got[g] = both.astype(BF).reshape(nb, 4 * kk, t)
        outs = []
        for odd in (0, 1):
            right = [lax.dynamic_index_in_dim(slabs[g], zl ^ odd, 0, False) for g in (0, 2, 4, 6)]
            right += [got[g] for g in ((1, 3, 5, 7) if odd else (0, 2, 4, 6))]
            right = jnp.stack(right)
            right = jnp.transpose(right, (0, 2, 1, 3)).reshape(32 * kk, nb * t)
            outs.append(dot(left[odd], right).astype(BF).reshape(4, rows, nb * t))
        out = jnp.stack(outs, axis=1)
        pieces = [out[0]] + [send(out[d], along("x", d)) for d in (1, 2, 3)]
        for n, b in enumerate(blocks):
            results[b] = [p[:, :, n * t : (n + 1) * t] for p in pieces]

    a8, yb, cb, s2, b8 = digits((u, 4, 2, 3, u))
    dd = (x - y - yb) % 4
    source = (((dd * 3 + s2) * u + a8) * 2 + cb) * u + b8
    gather = one_hot(source, 12 * t)
    final = []
    for s in range(3):
        wide = jnp.concatenate(
            [results[(s, q)][d] for d in range(4) for q in range(3)], axis=2
        )
        got = dot(wide.reshape(2 * rows, 12 * t), gather).astype(BF)
        final.append(got.reshape(2, rows, u, vb // 2))
    final = jnp.stack(final)
    final = jnp.where(zl == 0, final, final[:, ::-1])
    final = jnp.transpose(final, (2, 0, 3, 1, 4))
    return final.reshape(oi, oj, va, vb)


def solution(mesh):
    fine = Mesh(mesh.devices.reshape(SIZES), AXES)
    row, col = ("zh", "x"), ("zl", "y", "core")
    return jax.shard_map(
        per_device,
        mesh=fine,
        in_specs=(P(row, None, col), P(row, col, None)),
        out_specs=P(row, None, col, None),
        check_vma=False,
    )
```

```python
import functools

import jax
import jax.numpy as jnp
import numpy as np
from jax import lax
from jax.experimental import pallas as pl
from jax.experimental.pallas import tpu as pltpu
from jax.sharding import Mesh, PartitionSpec as P

AXES = ("zh", "x", "zl", "y", "core")
SIZES = (4, 4, 2, 4, 2)
BF = jnp.bfloat16
F32 = jnp.float32
CHUNKS = (((0, 2), (2, 0), (1, 2), (2, 1), (2, 2)), ((0, 0), (0, 1), (1, 0), (1, 1)))
GROUPS = ((0, 1, 7, 2, 6), (3, 5, 4))
GATE = 3


def pairs(move):
    out = []
    for i in range(256):
        here = dict(zip(AXES, (int(v) for v in np.unravel_index(i, SIZES))))
        there = move(dict(here))
        out.append((i, int(np.ravel_multi_index([there[a] for a in AXES], SIZES))))
    return out


def along_z(step):
    def move(d):
        z = (d["zh"] * 2 + d["zl"] + step) % 8
        d["zh"], d["zl"] = z // 2, z % 2
        return d

    return pairs(move)


def along(axis, step):
    size = SIZES[AXES.index(axis)]

    def move(d):
        d[axis] = (d[axis] + step) % size
        return d

    return pairs(move)


def mirror(d):
    d["y"] = (d["x"] - d["y"]) % 4
    return d


def send(value, table):
    return lax.ppermute(value, AXES, table)


def one_hot(source, rows):
    at = lax.broadcasted_iota(jnp.int32, (rows, source.shape[0]), 0)
    return (at == source[None, :]).astype(BF)


def digits(sizes):
    n = int(np.prod(sizes))
    return [jnp.asarray(v, jnp.int32) for v in np.unravel_index(np.arange(n), sizes)]


def dot(a, b):
    return jnp.dot(a, b, preferred_element_type=F32)


def whole(shape):
    zeros = (0,) * len(shape)
    return pl.BlockSpec(shape, lambda *_: zeros, pipeline_mode=pl.Buffered(1))


def product_kernel(turn, names, scalar, left, keep, *refs):
    slabs = {g: r for g, r in zip((0, 2, 6), refs[:3])}
    four = refs[3:5]
    n_groups = len(GROUPS)
    own_refs, other_refs = refs[5 : 5 + n_groups], refs[5 + n_groups : 5 + 2 * n_groups]
    out, right = refs[-2:]
    odd, d = pl.program_id(0), pl.program_id(1)
    zl, zh, core = scalar[0], scalar[1], scalar[2]
    nb, kt, t = slabs[0].shape[1:]
    half, part = zl ^ odd, kt // 2

    def place(base, at, i, value):
        for c in (0, 1):
            to = base + (c ^ core) * (4 * part) + at * part
            to = pl.ds(pl.multiple_of(to, part), part)
            right[to, i * t : (i + 1) * t] = value[c * part : (c + 1) * part]

    @pl.when(d == 0)
    def _():
        for n, g in enumerate((0, 2, 4, 6)):
            for i in range(nb):
                if g == 4:
                    v = jnp.where(half == 0, four[0][i], four[1][i])
                else:
                    v = slabs[g][half, i]
                place(0, lax.rem(zh + n, 4), i, v)

    for parity in (0, 1):

        @pl.when(jnp.logical_and(d == 0, odd == parity))
        def _(parity=parity):
            for n in range(4):
                group, m = names[2 * n + parity]
                for i in range(nb):
                    both = [r[group][m, turn[i]] for r in (own_refs, other_refs)]
                    both = dot(jnp.concatenate(both, axis=1), keep[...]).astype(BF)
                    place(4 * kt, lax.rem(zh + n + parity * zl, 4), i, both)

    out[0, 0] = dot(left[...], right[...]).astype(BF)


def product(scalars, left, keep, slabs, owns, others, turn):
    nb, kt, t = slabs[0].shape[1:]
    rows, depth = left.shape[0] // 4, left.shape[1]
    names = {g: (at, m) for at, group in enumerate(GROUPS) for m, g in enumerate(group)}
    arrays = [slabs[0], slabs[2], slabs[6], *slabs[4], *owns, *others]
    return pl.pallas_call(
        functools.partial(product_kernel, turn, names),
        out_shape=jax.ShapeDtypeStruct((4, 2, rows, nb * t), BF),
        grid_spec=pltpu.PrefetchScalarGridSpec(
            num_scalar_prefetch=1,
            grid=(2, 4),
            in_specs=[
                pl.BlockSpec((rows, depth), lambda o, d, _: (d, 0)),
                whole(keep.shape),
                *[whole(a.shape) for a in arrays],
            ],
            out_specs=pl.BlockSpec((1, 1, rows, nb * t), lambda o, d, _: (d, o, 0, 0)),
            scratch_shapes=[pltpu.VMEM((depth, nb * t), BF)],
        ),
        cost_estimate=pl.CostEstimate(
            flops=2 * 8 * rows * depth * nb * t,
            bytes_accessed=2 * sum(int(np.prod(a.shape)) for a in (left, *arrays)),
            transcendentals=0,
        ),
        compiler_params=pltpu.CompilerParams(dimension_semantics=("arbitrary", "arbitrary")),
    )(scalars, left, keep, *arrays)


def arrange_kernel(blocks, parts, adds, scalar, gather, pieces, *refs):
    out = refs[-1]
    zl = scalar[0]
    u = gather.shape[1] // 256
    wide = out.shape[1] // u
    t = gather.shape[0] // 12
    for s in parts:

        @pl.when(pl.program_id(0) == s)
        def _(s=s):
            mine = [q for q in range(3) if (s, q) in blocks]
            table = gather[mine[0] * 4 * t : (mine[-1] + 1) * 4 * t]
            z = []
            for half in (0, 1):
                tiles = []
                for q in mine:
                    n = blocks.index((s, q))
                    tiles += [pieces[d, zl ^ half, :, n * t : (n + 1) * t] for d in range(4)]
                z.append(dot(jnp.concatenate(tiles, axis=1), table))
            for r in range(u):
                low = z[0][:, r * 256 : (r + 1) * 256]
                high = pltpu.roll(z[1][:, r * 256 : (r + 1) * 256], 64, 1)
                for n, v in enumerate((low[:, :128], low[:, 128:] + high[:, :128], high[:, 128:])):
                    at = slice(r * wide + n * 128, r * wide + (n + 1) * 128)
                    v = v.astype(BF)
                    out[:, at] = v + refs[0][:, at] if adds else v


def arrange(scalars, gather, pieces, blocks, va, vb, before):
    rows, t = pieces.shape[2], gather.shape[0] // 12
    parts = sorted({s for s, _ in blocks})
    block = pl.BlockSpec((rows, va // 3 * vb), lambda s, _: (0, s))
    adds = before is not None
    return pl.pallas_call(
        functools.partial(arrange_kernel, blocks, parts, adds),
        out_shape=jax.ShapeDtypeStruct((rows, va * vb), BF),
        grid_spec=pltpu.PrefetchScalarGridSpec(
            num_scalar_prefetch=1,
            grid=(len(parts),),
            in_specs=[whole(gather.shape), whole(pieces.shape)] + [block] * adds,
            out_specs=block,
        ),
        input_output_aliases={3: 0} if adds else {},
        cost_estimate=pl.CostEstimate(
            flops=2 * 2 * rows * gather.shape[1] * 4 * t * len(blocks),
            bytes_accessed=2 * rows * va * vb,
            transcendentals=0,
        ),
        compiler_params=pltpu.CompilerParams(dimension_semantics=("arbitrary",)),
    )(scalars, gather, pieces, *([before] if adds else []))


def left_kernel(oi, own, other, out):
    rows, depth = own.shape[1] // 2, own.shape[2]
    for n, given in enumerate((own, other)):
        direct = slice(n * depth, (n + 1) * depth)
        turned = slice((2 + n) * depth, (3 + n) * depth)
        for xi in range(4):
            out[xi * rows : (xi + 1) * rows, direct] = given[xi, :rows, :]
            for i in range(oi):
                run = 4 * oi
                at = rows + (xi * oi + i) * run
                blocks = [given[xj, at : at + run, :].astype(F32) for xj in range(4)]
                order = [blocks[xj][z * oi : (z + 1) * oi] for z in range(4) for xj in range(4)]
                to = xi * rows + i * 4 * run
                out[to : to + 4 * run, turned] = jnp.concatenate(order, axis=0).astype(BF)


def amplitude_columns(amplitudes):
    oi, oj, kk = amplitudes.shape
    rows = oi * oj
    direct = jnp.transpose(amplitudes, (2, 0, 1)).reshape(kk, rows)
    turned = amplitudes.reshape(oi, 4, 4 * oi, kk)
    turned = lax.all_to_all(jnp.transpose(turned, (1, 3, 0, 2)), "zh", 0, 0, tiled=True)
    turned = jnp.transpose(turned, (1, 3, 0, 2)).reshape(kk, rows)
    amp = jnp.concatenate([direct, turned], axis=1)
    return jnp.broadcast_to(amp[None], (8, kk, 2 * rows))


def amplitude_rows(amp, oi):
    amp = lax.all_to_all(amp, ("zl", "y"), 0, 0, tiled=True)
    both = amp.shape[2]
    amp = jnp.transpose(amp.reshape(-1, both))
    amp = jnp.broadcast_to(amp[None], (4, *amp.shape))
    amp = lax.all_to_all(amp, "x", 0, 0, tiled=True)
    other = send(amp, along("core", 1))
    return pl.pallas_call(
        functools.partial(left_kernel, oi),
        out_shape=jax.ShapeDtypeStruct((2 * both, 4 * amp.shape[2]), BF),
        in_specs=[pl.BlockSpec(memory_space=pltpu.VMEM)] * 2,
        out_specs=pl.BlockSpec(memory_space=pltpu.VMEM),
        cost_estimate=pl.CostEstimate(flops=0, bytes_accessed=16 * both * amp.shape[2], transcendentals=0),
    )(amp, other)


def per_device(amplitudes, integrals):
    oi, oj, kk = amplitudes.shape
    va, vb = integrals.shape[1:]
    u = va // 3
    t = 2 * u * u
    zh, x, zl, y, core = (lax.axis_index(a) for a in AXES)
    scalars = jnp.stack([zl, zh, core])

    dx, s2, a8, cb, b8 = digits((4, 3, u, 2, u))
    yb = (dx - y) % 4
    source = (((a8 * 4 + yb) * 2 + cb) * 3 + s2) * u + b8
    spread = one_hot(source, 12 * t)
    v = integrals.reshape(kk, 3, u, 2, vb // 2)
    v = jnp.transpose(v, (3, 1, 0, 2, 4)).reshape(6 * kk, u * vb // 2)
    v, amplitudes = lax.optimization_barrier((v, amplitudes))
    v = dot(v, spread).astype(BF)
    v = v.reshape(2, 3, kk, 4, 3, t)
    v = jnp.transpose(v, (3, 0, 1, 4, 2, 5))
    v = lax.all_to_all(v.reshape(4, -1, t), "x", 0, 0, tiled=True)
    amp = amplitude_columns(amplitudes)
    v, amp = lax.optimization_barrier((v, amp))
    left = amplitude_rows(amp, oi)
    v = v.reshape(4, 2, 3, 3, kk, t)

    a8, cb, b8 = digits((u, 2, u))
    place = (b8 * 2 + core) * u + a8
    keep = one_hot(jnp.where(cb == core, place, t + place), 2 * t)

    a8, lane = digits((u, 256))
    yb, rest = lane // (6 * u), lane % (6 * u)
    cb, s2, b8 = rest // (3 * u), rest // u % 3, rest % u
    source = ((((s2 * 4 + (yb + y) % 4) * u) + a8) * 2 + cb) * u + b8
    gather = one_hot(jnp.where(lane < 24 * u, source, -1), 12 * t)

    done, gate = [], None
    for c, blocks in enumerate(CHUNKS):
        nb = len(blocks)
        slab = jnp.stack([v[:, :, s, q] for s, q in blocks], axis=2).reshape(2, 2, 2, nb, kk, t)
        slab = jnp.transpose(slab, (2, 3, 1, 0, 4, 5)).reshape(2, nb, 4 * kk, t)
        if c > 0:
            slab, _ = lax.optimization_barrier((slab, gate))
        slabs = {0: slab}
        up = down = slab
        for step in (1, 2, 3):
            up, down = send(up, along_z(1)), send(down, along_z(-1))
            slabs[8 - step], slabs[step] = up, down
            if step == GATE:
                gate = up
        if c > 0:
            up, down, _ = lax.optimization_barrier((up, down, done[-1][1]))
        slabs[4] = (send(up[0], along_z(1)), send(down[1], along_z(-1)))
        owns, others = [], []
        for group in GROUPS:
            part = [
                jnp.where(zl == 0, *slabs[g]) if g == 4 else lax.dynamic_index_in_dim(slabs[g], zl, 0, False)
                for g in group
            ]
            part = send(jnp.stack(part), pairs(mirror))
            owns.append(part)
            others.append(send(part, along("core", 1)))
        turn = [blocks.index((q, s)) for s, q in blocks]
        out = product(scalars, left, keep, slabs, owns, others, turn)
        done.append((blocks, out, lax.all_to_all(out, "x", 0, 0, tiled=True)))

    final = None
    for c, (blocks, out, pieces) in enumerate(done):
        if c + 1 < len(done):
            pieces, _ = lax.optimization_barrier((pieces, done[c + 1][1]))
        final = arrange(scalars, gather, pieces, blocks, va, vb, final)
    return final.reshape(oi, oj, va, vb)


def solution(mesh):
    fine = Mesh(mesh.devices.reshape(SIZES), AXES)
    row, col = ("zh", "x"), ("zl", "y", "core")
    return jax.shard_map(
        per_device,
        mesh=fine,
        in_specs=(P(row, None, col), P(row, col, None)),
        out_specs=P(row, None, col, None),
        check_vma=False,
    )
```

```python
import functools

import jax
import jax.numpy as jnp
import numpy as np
from jax import lax
from jax.experimental import pallas as pl
from jax.experimental.pallas import tpu as pltpu
from jax.sharding import Mesh, PartitionSpec as P

AXES = ("zh", "x", "zl", "y", "core")
SIZES = (4, 4, 2, 4, 2)
BF = jnp.bfloat16
F32 = jnp.float32
SETS = (((0, 0), (0, 1), (1, 0)), ((1, 1), (0, 2), (2, 0)), ((2, 2), (1, 2), (2, 1)))
GROUPS = ((0,), (1, 7), (2, 6), (3, 5), (4,))


def pairs(move):
    out = []
    for i in range(256):
        here = dict(zip(AXES, (int(v) for v in np.unravel_index(i, SIZES))))
        there = move(dict(here))
        out.append((i, int(np.ravel_multi_index([there[a] for a in AXES], SIZES))))
    return out


def along_z(step):
    def move(d):
        z = (d["zh"] * 2 + d["zl"] + step) % 8
        d["zh"], d["zl"] = z // 2, z % 2
        return d

    return pairs(move)


def along(axis, step):
    size = SIZES[AXES.index(axis)]

    def move(d):
        d[axis] = (d[axis] + step) % size
        return d

    return pairs(move)


def mirror(d):
    d["y"] = (d["x"] - d["y"]) % 4
    return d


def send(value, table):
    return lax.ppermute(value, AXES, table)


def one_hot(source, rows):
    at = lax.broadcasted_iota(jnp.int32, (rows, source.shape[0]), 0)
    return (at == source[None, :]).astype(BF)


def digits(sizes):
    n = int(np.prod(sizes))
    return [jnp.asarray(v, jnp.int32) for v in np.unravel_index(np.arange(n), sizes)]


def dot(a, b):
    return jnp.dot(a, b, preferred_element_type=F32)


def whole(shape):
    zeros = (0,) * len(shape)
    return pl.BlockSpec(shape, lambda *_: zeros, pipeline_mode=pl.Buffered(1))


def of_set(shape, nb, at):
    front = (0,) * (len(shape) - 3)
    return pl.BlockSpec(
        (*shape[:-3], nb, *shape[-2:]), lambda *_: (*front, at, 0, 0), pipeline_mode=pl.Buffered(1)
    )


def product_kernel(turn, names, scalar, left, keep, *refs):
    slabs = {g: r for g, r in zip((0, 2, 6), refs[:3])}
    four = refs[3:5]
    n_groups = len(GROUPS)
    own_refs, other_refs = refs[5 : 5 + n_groups], refs[5 + n_groups : 5 + 2 * n_groups]
    out, right = refs[-2:]
    odd, d = pl.program_id(0), pl.program_id(1)
    zl, zh, core = scalar[0], scalar[1], scalar[2]
    nb, kt, t = slabs[0].shape[1:]
    half, part = zl ^ odd, kt // 2

    def place(base, at, i, value):
        for c in (0, 1):
            to = base + (c ^ core) * (4 * part) + at * part
            to = pl.ds(pl.multiple_of(to, part), part)
            right[to, i * t : (i + 1) * t] = value[c * part : (c + 1) * part]

    @pl.when(d == 0)
    def _():
        for n, g in enumerate((0, 2, 4, 6)):
            for i in range(nb):
                if g == 4:
                    v = jnp.where(half == 0, four[0][i], four[1][i])
                else:
                    v = slabs[g][half, i]
                place(0, lax.rem(zh + n, 4), i, v)

    for parity in (0, 1):

        @pl.when(jnp.logical_and(d == 0, odd == parity))
        def _(parity=parity):
            for n in range(4):
                group, m = names[2 * n + parity]
                for i in range(nb):
                    both = [r[group][m, turn[i]] for r in (own_refs, other_refs)]
                    both = dot(jnp.concatenate(both, axis=1), keep[...]).astype(BF)
                    place(4 * kt, lax.rem(zh + n + parity * zl, 4), i, both)

    out[0, 0] = dot(left[...], right[...]).astype(BF)


def product(scalars, left, keep, slabs, owns, others, turn, at):
    _, kt, t = slabs[0].shape[1:]
    nb = len(turn)
    rows, depth = left.shape[0] // 4, left.shape[1]
    names = {g: (at, m) for at, group in enumerate(GROUPS) for m, g in enumerate(group)}
    arrays = [slabs[0], slabs[2], slabs[6], *slabs[4], *owns, *others]
    return pl.pallas_call(
        functools.partial(product_kernel, turn, names),
        out_shape=jax.ShapeDtypeStruct((4, 2, rows, nb * t), BF),
        grid_spec=pltpu.PrefetchScalarGridSpec(
            num_scalar_prefetch=1,
            grid=(2, 4),
            in_specs=[
                pl.BlockSpec((rows, depth), lambda o, d, _: (d, 0)),
                whole(keep.shape),
                *[of_set(a.shape, nb, at) for a in arrays],
            ],
            out_specs=pl.BlockSpec((1, 1, rows, nb * t), lambda o, d, _: (d, o, 0, 0)),
            scratch_shapes=[pltpu.VMEM((depth, nb * t), BF)],
        ),
        cost_estimate=pl.CostEstimate(
            flops=2 * 8 * rows * depth * nb * t,
            bytes_accessed=4 * left.size + 2 * nb * kt * t * 24,
            transcendentals=0,
        ),
        compiler_params=pltpu.CompilerParams(dimension_semantics=("arbitrary", "arbitrary")),
    )(scalars, left, keep, *arrays)


def arrange_kernel(blocks, parts, adds, scalar, gather, pieces, *refs):
    out = refs[-1]
    zl = scalar[0]
    u = gather.shape[1] // 256
    wide = out.shape[1] // u
    t = gather.shape[0] // 12
    for s in parts:

        @pl.when(pl.program_id(0) == s - parts[0])
        def _(s=s):
            mine = [q for q in range(3) if (s, q) in blocks]
            table = gather[mine[0] * 4 * t : (mine[-1] + 1) * 4 * t]
            z = []
            for half in (0, 1):
                tiles = []
                for q in mine:
                    n = blocks.index((s, q))
                    tiles += [pieces[d, zl ^ half, :, n * t : (n + 1) * t] for d in range(4)]
                z.append(dot(jnp.concatenate(tiles, axis=1), table))
            for r in range(u):
                low = z[0][:, r * 256 : (r + 1) * 256]
                high = pltpu.roll(z[1][:, r * 256 : (r + 1) * 256], 64, 1)
                for n, v in enumerate((low[:, :128], low[:, 128:] + high[:, :128], high[:, 128:])):
                    at = slice(r * wide + n * 128, r * wide + (n + 1) * 128)
                    v = v.astype(BF)
                    out[:, at] = v + refs[0][:, at] if s in adds else v


def arrange(scalars, gather, pieces, blocks, va, vb, before, seen):
    rows, t = pieces.shape[2], gather.shape[0] // 12
    parts = sorted({s for s, _ in blocks})
    block = pl.BlockSpec((rows, va // 3 * vb), lambda s, _: (0, s + parts[0]))
    more = before is not None
    return pl.pallas_call(
        functools.partial(arrange_kernel, blocks, parts, [s for s in parts if s in seen]),
        out_shape=jax.ShapeDtypeStruct((rows, va * vb), BF),
        grid_spec=pltpu.PrefetchScalarGridSpec(
            num_scalar_prefetch=1,
            grid=(len(parts),),
            in_specs=[whole(gather.shape), whole(pieces.shape)] + [block] * more,
            out_specs=block,
        ),
        input_output_aliases={3: 0} if more else {},
        cost_estimate=pl.CostEstimate(
            flops=2 * 2 * rows * gather.shape[1] * 4 * t * len(blocks),
            bytes_accessed=2 * rows * va * vb,
            transcendentals=0,
        ),
        compiler_params=pltpu.CompilerParams(dimension_semantics=("arbitrary",)),
    )(scalars, gather, pieces, *([before] if more else []))


def left_kernel(oi, own, other, out):
    rows, depth = own.shape[1] // 2, own.shape[2]
    for n, given in enumerate((own, other)):
        direct = slice(n * depth, (n + 1) * depth)
        turned = slice((2 + n) * depth, (3 + n) * depth)
        for xi in range(4):
            out[xi * rows : (xi + 1) * rows, direct] = given[xi, :rows, :]
            for i in range(oi):
                run = 4 * oi
                at = rows + (xi * oi + i) * run
                blocks = [given[xj, at : at + run, :].astype(F32) for xj in range(4)]
                order = [blocks[xj][z * oi : (z + 1) * oi] for z in range(4) for xj in range(4)]
                to = xi * rows + i * 4 * run
                out[to : to + 4 * run, turned] = jnp.concatenate(order, axis=0).astype(BF)


def amplitude_columns(amplitudes):
    oi, oj, kk = amplitudes.shape
    rows = oi * oj
    direct = jnp.transpose(amplitudes, (2, 0, 1)).reshape(kk, rows)
    turned = amplitudes.reshape(oi, 4, 4 * oi, kk)
    turned = lax.all_to_all(jnp.transpose(turned, (1, 3, 0, 2)), "zh", 0, 0, tiled=True)
    turned = jnp.transpose(turned, (1, 3, 0, 2)).reshape(kk, rows)
    amp = jnp.concatenate([direct, turned], axis=1)
    return jnp.broadcast_to(amp[None], (8, kk, 2 * rows))


def amplitude_rows(amp, oi):
    amp = lax.all_to_all(amp, ("zl", "y"), 0, 0, tiled=True)
    both = amp.shape[2]
    amp = jnp.transpose(amp.reshape(-1, both))
    amp = jnp.broadcast_to(amp[None], (4, *amp.shape))
    amp = lax.all_to_all(amp, "x", 0, 0, tiled=True)
    other = send(amp, along("core", 1))
    return pl.pallas_call(
        functools.partial(left_kernel, oi),
        out_shape=jax.ShapeDtypeStruct((2 * both, 4 * amp.shape[2]), BF),
        in_specs=[pl.BlockSpec(memory_space=pltpu.VMEM)] * 2,
        out_specs=pl.BlockSpec(memory_space=pltpu.VMEM),
        cost_estimate=pl.CostEstimate(flops=0, bytes_accessed=16 * both * amp.shape[2], transcendentals=0),
    )(amp, other)


def per_device(amplitudes, integrals):
    oi, oj, kk = amplitudes.shape
    va, vb = integrals.shape[1:]
    u = va // 3
    t = 2 * u * u
    zh, x, zl, y, core = (lax.axis_index(a) for a in AXES)
    scalars = jnp.stack([zl, zh, core])

    dx, s2, a8, cb, b8 = digits((4, 3, u, 2, u))
    yb = (dx - y) % 4
    source = (((a8 * 4 + yb) * 2 + cb) * 3 + s2) * u + b8
    spread = one_hot(source, 12 * t)
    v = integrals.reshape(kk, 3, u, 2, vb // 2)
    v = jnp.transpose(v, (3, 1, 0, 2, 4)).reshape(6 * kk, u * vb // 2)
    v = dot(v, spread).astype(BF)
    v = v.reshape(2, 3, kk, 4, 3, t)
    v = jnp.transpose(v, (3, 0, 1, 4, 2, 5))
    amp = amplitude_columns(amplitudes)
    v, amp = lax.optimization_barrier((v, amp))
    v = lax.all_to_all(v.reshape(4, -1, t), "x", 0, 0, tiled=True)
    left = amplitude_rows(amp, oi)
    v = v.reshape(4, 2, 3, 3, kk, t)

    a8, cb, b8 = digits((u, 2, u))
    place = (b8 * 2 + core) * u + a8
    keep = one_hot(jnp.where(cb == core, place, t + place), 2 * t)

    a8, lane = digits((u, 256))
    yb, rest = lane // (6 * u), lane % (6 * u)
    cb, s2, b8 = rest // (3 * u), rest // u % 3, rest % u
    source = ((((s2 * 4 + (yb + y) % 4) * u) + a8) * 2 + cb) * u + b8
    gather = one_hot(jnp.where(lane < 24 * u, source, -1), 12 * t)

    left, gather, keep = lax.optimization_barrier((left, gather, keep))
    tiles = [b for blocks in SETS for b in blocks]
    slab = jnp.stack([v[:, :, s, q] for s, q in tiles], axis=2).reshape(2, 2, 2, 9, kk, t)
    slab = jnp.transpose(slab, (2, 3, 1, 0, 4, 5)).reshape(2, 9, 4 * kk, t)
    slabs = {0: slab}
    up = down = slab
    for step in (1, 2, 3):
        up, down = send(up, along_z(1)), send(down, along_z(-1))
        slabs[8 - step], slabs[step] = up, down
    slabs[4] = (send(up[0], along_z(1)), send(down[1], along_z(-1)))
    owns, others = [], []
    for group in GROUPS:
        part = [
            jnp.where(zl == 0, *slabs[g]) if g == 4 else lax.dynamic_index_in_dim(slabs[g], zl, 0, False)
            for g in group
        ]
        part = send(jnp.stack(part), pairs(mirror))
        owns.append(part)
        others.append(send(part, along("core", 1)))
    done = []
    for c, blocks in enumerate(SETS):
        turn = [blocks.index((q, s)) for s, q in blocks]
        if c == 1:
            left, _ = lax.optimization_barrier((left, done[0][1]))
        if c == 2:
            left, _ = lax.optimization_barrier((left, done[0][2]))
        out = product(scalars, left, keep, slabs, owns, others, turn, c)
        if done:
            out, _ = lax.optimization_barrier((out, done[-1][2]))
        done.append((blocks, out, lax.all_to_all(out, "x", 0, 0, tiled=True)))

    final, seen = None, set()
    for c, (blocks, out, pieces) in enumerate(done):
        if c == 0:
            pieces, _ = lax.optimization_barrier((pieces, done[-1][1]))
        final = arrange(scalars, gather, pieces, blocks, va, vb, final, seen)
        seen |= {s for s, _ in blocks}
    return final.reshape(oi, oj, va, vb)


def solution(mesh):
    fine = Mesh(mesh.devices.reshape(SIZES), AXES)
    row, col = ("zh", "x"), ("zl", "y", "core")
    return jax.shard_map(
        per_device,
        mesh=fine,
        in_specs=(P(row, None, col), P(row, col, None)),
        out_specs=P(row, None, col, None),
        check_vma=False,
    )
```

```python
import functools

import jax
import jax.numpy as jnp
import numpy as np
from jax import lax
from jax.experimental import pallas as pl
from jax.experimental.pallas import tpu as pltpu
from jax.sharding import Mesh, PartitionSpec as P

AXES = ("zh", "x", "zl", "y", "core")
SIZES = (4, 4, 2, 4, 2)
BF = jnp.bfloat16
F32 = jnp.float32
TILES = tuple((s, q) for s in range(3) for q in range(3))
GROUPS = ((0,), (1, 7), (2, 6), (3, 5), (4,))


def pairs(move):
    out = []
    for i in range(256):
        here = dict(zip(AXES, (int(v) for v in np.unravel_index(i, SIZES))))
        there = move(dict(here))
        out.append((i, int(np.ravel_multi_index([there[a] for a in AXES], SIZES))))
    return out


def along_z(step):
    def move(d):
        z = (d["zh"] * 2 + d["zl"] + step) % 8
        d["zh"], d["zl"] = z // 2, z % 2
        return d

    return pairs(move)


def along(axis, step):
    size = SIZES[AXES.index(axis)]

    def move(d):
        d[axis] = (d[axis] + step) % size
        return d

    return pairs(move)


def mirror(d):
    d["y"] = (d["x"] - d["y"]) % 4
    return d


def send(value, table):
    return lax.ppermute(value, AXES, table)


def one_hot(source, rows):
    at = lax.broadcasted_iota(jnp.int32, (rows, source.shape[0]), 0)
    return (at == source[None, :]).astype(BF)


def digits(sizes):
    n = int(np.prod(sizes))
    return [jnp.asarray(v, jnp.int32) for v in np.unravel_index(np.arange(n), sizes)]


def dot(a, b):
    return jnp.dot(a, b, preferred_element_type=F32)


def whole(shape):
    zeros = (0,) * len(shape)
    return pl.BlockSpec(shape, lambda *_: zeros, pipeline_mode=pl.Buffered(1))


def product_kernel(turn, names, scalar, left, keep, *refs):
    slabs = {g: r for g, r in zip((0, 2, 6), refs[:3])}
    four = refs[3:5]
    n_groups = len(GROUPS)
    own_refs, other_refs = refs[5 : 5 + n_groups], refs[5 + n_groups : 5 + 2 * n_groups]
    outs, right = refs[-5:-1], refs[-1]
    odd, d = pl.program_id(0), pl.program_id(1)
    zl, zh, core = scalar[0], scalar[1], scalar[2]
    nb, kt, t = slabs[0].shape[1:]
    half, part = zl ^ odd, kt // 2

    def place(base, at, i, value):
        for c in (0, 1):
            to = base + (c ^ core) * (4 * part) + at * part
            to = pl.ds(pl.multiple_of(to, part), part)
            right[to, i * t : (i + 1) * t] = value[c * part : (c + 1) * part]

    @pl.when(d == 0)
    def _():
        for n, g in enumerate((0, 2, 4, 6)):
            for i in range(nb):
                if g == 4:
                    v = jnp.where(half == 0, four[0][i], four[1][i])
                else:
                    v = slabs[g][half, i]
                place(0, lax.rem(zh + n, 4), i, v)

    for parity in (0, 1):

        @pl.when(jnp.logical_and(d == 0, odd == parity))
        def _(parity=parity):
            for n in range(4):
                group, m = names[2 * n + parity]
                for i in range(nb):
                    both = [r[group][m, turn[i]] for r in (own_refs, other_refs)]
                    both = dot(jnp.concatenate(both, axis=1), keep[...]).astype(BF)
                    place(4 * kt, lax.rem(zh + n + parity * zl, 4), i, both)

    value = dot(left[...], right[...]).astype(BF)
    for to, out in enumerate(outs):

        @pl.when(d == to)
        def _(out=out):
            out[0] = value


def product(scalars, left, keep, slabs, owns, others, turn):
    _, nb, kt, t = slabs[0].shape
    rows, depth = left.shape[0] // 4, left.shape[1]
    names = {g: (at, m) for at, group in enumerate(GROUPS) for m, g in enumerate(group)}
    arrays = [slabs[0], slabs[2], slabs[6], *slabs[4], *owns, *others]
    return pl.pallas_call(
        functools.partial(product_kernel, turn, names),
        out_shape=[jax.ShapeDtypeStruct((2, rows, nb * t), BF)] * 4,
        grid_spec=pltpu.PrefetchScalarGridSpec(
            num_scalar_prefetch=1,
            grid=(2, 4),
            in_specs=[
                pl.BlockSpec((rows, depth), lambda o, d, _: (d, 0)),
                whole(keep.shape),
                *[whole(a.shape) for a in arrays],
            ],
            out_specs=[pl.BlockSpec((1, rows, nb * t), lambda o, d, _: (o, 0, 0))] * 4,
            scratch_shapes=[pltpu.VMEM((depth, nb * t), BF)],
        ),
        cost_estimate=pl.CostEstimate(
            flops=2 * 8 * rows * depth * nb * t,
            bytes_accessed=2 * left.size + 2 * nb * kt * t * 24,
            transcendentals=0,
        ),
        compiler_params=pltpu.CompilerParams(dimension_semantics=("arbitrary", "arbitrary")),
    )(scalars, left, keep, *arrays)


def arrange_kernel(given, adds, scalar, gather, *refs):
    pieces, out = refs[: len(given)], refs[-1]
    zl = scalar[0]
    u = gather.shape[1] // 256
    wide = out.shape[1] // u
    t = gather.shape[0] // 12
    table = gather[given[0] * 3 * t : (given[-1] + 1) * 3 * t]
    for s in range(3):

        @pl.when(pl.program_id(0) == s)
        def _(s=s):
            z = []
            for half in (0, 1):
                tiles = [p[zl ^ half, :, s * 3 * t : (s + 1) * 3 * t] for p in pieces]
                z.append(dot(jnp.concatenate(tiles, axis=1), table))
            for r in range(u):
                low = z[0][:, r * 256 : (r + 1) * 256]
                high = pltpu.roll(z[1][:, r * 256 : (r + 1) * 256], 64, 1)
                for n, v in enumerate((low[:, :128], low[:, 128:] + high[:, :128], high[:, 128:])):
                    at = slice(r * wide + n * 128, r * wide + (n + 1) * 128)
                    v = v.astype(BF)
                    out[:, at] = v + refs[len(given)][:, at] if adds else v


def arrange(scalars, gather, pieces, given, va, vb, before):
    rows, t = pieces[0].shape[1], gather.shape[0] // 12
    block = pl.BlockSpec((rows, va // 3 * vb), lambda s, _: (0, s))
    adds = before is not None
    return pl.pallas_call(
        functools.partial(arrange_kernel, given, adds),
        out_shape=jax.ShapeDtypeStruct((rows, va * vb), BF),
        grid_spec=pltpu.PrefetchScalarGridSpec(
            num_scalar_prefetch=1,
            grid=(3,),
            in_specs=[whole(gather.shape)] + [whole(p.shape) for p in pieces] + [block] * adds,
            out_specs=block,
        ),
        input_output_aliases={2 + len(given): 0} if adds else {},
        cost_estimate=pl.CostEstimate(
            flops=2 * 18 * rows * gather.shape[1] * t * len(given),
            bytes_accessed=2 * rows * va * vb,
            transcendentals=0,
        ),
        compiler_params=pltpu.CompilerParams(dimension_semantics=("arbitrary",)),
    )(scalars, gather, *pieces, *([before] if adds else []))


def left_kernel(oi, scalar, own, other, out):
    rows, depth = own.shape[1] // 2, own.shape[2]
    run = 4 * oi
    for n, given in enumerate((own, other)):
        direct = slice(n * depth, (n + 1) * depth)
        turned = slice((2 + n) * depth, (3 + n) * depth)
        for d in range(4):
            xi = lax.rem(scalar[3] + d, 4)
            out[d * rows : (d + 1) * rows, direct] = given[xi, :rows, :]
            for i in range(oi):
                at = pl.ds(pl.multiple_of(rows + (xi * oi + i) * run, run), run)
                blocks = [given[xj, at, :].astype(F32) for xj in range(4)]
                order = [blocks[xj][z * oi : (z + 1) * oi] for z in range(4) for xj in range(4)]
                to = d * rows + i * 4 * run
                out[to : to + 4 * run, turned] = jnp.concatenate(order, axis=0).astype(BF)


def amplitude_columns(amplitudes):
    oi, oj, kk = amplitudes.shape
    rows = oi * oj
    direct = jnp.transpose(amplitudes, (2, 0, 1)).reshape(kk, rows)
    turned = amplitudes.reshape(oi, 4, 4 * oi, kk)
    turned = lax.all_to_all(jnp.transpose(turned, (1, 3, 0, 2)), "zh", 0, 0, tiled=True)
    turned = jnp.transpose(turned, (1, 3, 0, 2)).reshape(kk, rows)
    amp = jnp.concatenate([direct, turned], axis=1)
    return jnp.broadcast_to(amp[None], (8, kk, 2 * rows))


def amplitude_rows(scalars, amp, oi):
    amp = lax.all_to_all(amp, ("zl", "y"), 0, 0, tiled=True)
    both = amp.shape[2]
    amp = jnp.transpose(amp.reshape(-1, both))
    amp = jnp.broadcast_to(amp[None], (4, *amp.shape))
    amp = lax.all_to_all(amp, "x", 0, 0, tiled=True)
    other = send(amp, along("core", 1))
    shape = (2 * both, 4 * amp.shape[2])
    return pl.pallas_call(
        functools.partial(left_kernel, oi),
        out_shape=jax.ShapeDtypeStruct(shape, BF),
        grid_spec=pltpu.PrefetchScalarGridSpec(
            num_scalar_prefetch=1,
            grid=(1,),
            in_specs=[whole(amp.shape)] * 2,
            out_specs=whole(shape),
        ),
        cost_estimate=pl.CostEstimate(flops=0, bytes_accessed=16 * both * amp.shape[2], transcendentals=0),
    )(scalars, amp, other)


def per_device(amplitudes, integrals):
    oi, oj, kk = amplitudes.shape
    va, vb = integrals.shape[1:]
    u = va // 3
    t = 2 * u * u
    zh, x, zl, y, core = (lax.axis_index(a) for a in AXES)
    scalars = jnp.stack([zl, zh, core, x])

    dx, s2, a8, cb, b8 = digits((4, 3, u, 2, u))
    yb = (dx - y) % 4
    source = (((a8 * 4 + yb) * 2 + cb) * 3 + s2) * u + b8
    spread = one_hot(source, 12 * t)
    v = integrals.reshape(kk, 3, u, 2, vb // 2)
    v = jnp.transpose(v, (3, 1, 0, 2, 4)).reshape(6 * kk, u * vb // 2)
    v = dot(v, spread).astype(BF)
    v = v.reshape(2, 3, kk, 4, 3, t)
    v = jnp.transpose(v, (3, 0, 1, 4, 2, 5))
    amp = amplitude_columns(amplitudes)
    v, amp = lax.optimization_barrier((v, amp))
    v = lax.all_to_all(v.reshape(4, -1, t), "x", 0, 0, tiled=True)
    left = amplitude_rows(scalars, amp, oi)
    v = v.reshape(4, 2, 3, 3, kk, t)

    a8, cb, b8 = digits((u, 2, u))
    place = (b8 * 2 + core) * u + a8
    keep = one_hot(jnp.where(cb == core, place, t + place), 2 * t)

    a8, lane = digits((u, 256))
    yb, rest = lane // (6 * u), lane % (6 * u)
    cb, s2, b8 = rest // (3 * u), rest // u % 3, rest % u
    source = (((((x - y - yb) % 4 * 3 + s2) * u) + a8) * 2 + cb) * u + b8
    gather = one_hot(jnp.where(lane < 24 * u, source, -1), 12 * t)

    slab = jnp.transpose(v.reshape(2, 2, 2, 9, kk, t), (2, 3, 1, 0, 4, 5)).reshape(2, 9, 4 * kk, t)
    slabs = {0: slab}
    up = down = slab
    owns, others = [], []

    def reflect(group):
        part = [
            jnp.where(zl == 0, *slabs[g]) if g == 4 else lax.dynamic_index_in_dim(slabs[g], zl, 0, False)
            for g in group
        ]
        part = send(jnp.stack(part), pairs(mirror))
        owns.append(part)
        others.append(send(part, along("core", 1)))

    for step, group in zip((1, 2, 3), GROUPS):
        up, down = send(up, along_z(1)), send(down, along_z(-1))
        reflect(group)
        slabs[8 - step], slabs[step] = up, down
        up, down, _ = lax.optimization_barrier((up, down, owns[-1]))
    slabs[4] = (send(up[0], along_z(1)), send(down[1], along_z(-1)))
    for group in GROUPS[3:]:
        reflect(group)
    turn = [TILES.index((q, s)) for s, q in TILES]
    outs = product(scalars, left, keep, slabs, owns, others, turn)
    away = {d: send(outs[d], along("x", d)) for d in (1, 3, 2)}
    final = arrange(scalars, gather, [outs[0], away[1]], (0, 1), va, vb, None)
    final = arrange(scalars, gather, [away[2], away[3]], (2, 3), va, vb, final)
    return final.reshape(oi, oj, va, vb)


def solution(mesh):
    fine = Mesh(mesh.devices.reshape(SIZES), AXES)
    row, col = ("zh", "x"), ("zl", "y", "core")
    return jax.shard_map(
        per_device,
        mesh=fine,
        in_specs=(P(row, None, col), P(row, col, None)),
        out_specs=P(row, None, col, None),
        check_vma=False,
    )
```

```python
import functools

import jax
import jax.numpy as jnp
import numpy as np
from jax import lax
from jax.experimental import pallas as pl
from jax.experimental.pallas import tpu as pltpu
from jax.sharding import Mesh, PartitionSpec as P

AXES = ("zh", "x", "zl", "y", "core")
SIZES = (4, 4, 2, 4, 2)
BF = jnp.bfloat16
F32 = jnp.float32
TILES = tuple((s, q) for s in range(3) for q in range(3))
GROUPS = ((0,), (1, 7), (2, 6), (3, 5), (4,))


def pairs(move):
    out = []
    for i in range(256):
        here = dict(zip(AXES, (int(v) for v in np.unravel_index(i, SIZES))))
        there = move(dict(here))
        out.append((i, int(np.ravel_multi_index([there[a] for a in AXES], SIZES))))
    return out


def along_z(step):
    def move(d):
        z = (d["zh"] * 2 + d["zl"] + step) % 8
        d["zh"], d["zl"] = z // 2, z % 2
        return d

    return pairs(move)


def along(axis, step):
    size = SIZES[AXES.index(axis)]

    def move(d):
        d[axis] = (d[axis] + step) % size
        return d

    return pairs(move)


def mirror(odd):
    def move(d):
        d["y"] = (d["x"] - d["y"] - 2 * odd) % 4
        return d

    return pairs(move)


def send(value, table):
    return lax.ppermute(value, AXES, table)


def one_hot(source, rows):
    at = lax.broadcasted_iota(jnp.int32, (rows, source.shape[0]), 0)
    return (at == source[None, :]).astype(BF)


def digits(sizes):
    n = int(np.prod(sizes))
    return [jnp.asarray(v, jnp.int32) for v in np.unravel_index(np.arange(n), sizes)]


def dot(a, b):
    return jnp.dot(a, b, preferred_element_type=F32)


def whole(shape):
    zeros = (0,) * len(shape)
    return pl.BlockSpec(shape, lambda *_: zeros, pipeline_mode=pl.Buffered(1))


def product_kernel(turn, names, scalar, left, keep, *refs):
    slabs = {g: r for g, r in zip((0, 2, 6), refs[:3])}
    four = refs[3:5]
    n_groups = 2 * len(GROUPS)
    own_refs, other_refs = refs[5 : 5 + n_groups], refs[5 + n_groups : 5 + 2 * n_groups]
    outs, right = refs[-5:-1], refs[-1]
    odd, d = pl.program_id(0), pl.program_id(1)
    zl, zh, core = scalar[0], scalar[1], scalar[2]
    nb, kt, t = slabs[0].shape[1:]
    half, part = zl ^ odd, kt // 2

    def place(base, at, i, value):
        for c in (0, 1):
            to = base + (c ^ core) * (4 * part) + at * part
            to = pl.ds(pl.multiple_of(to, part), part)
            right[to, i * t : (i + 1) * t] = value[c * part : (c + 1) * part]

    @pl.when(d == 0)
    def _():
        for n, g in enumerate((0, 2, 4, 6)):
            for i in range(nb):
                if g == 4:
                    v = jnp.where(half == 0, four[0][i], four[1][i])
                else:
                    v = slabs[g][half, i]
                place(0, lax.rem(zh + n, 4), i, v)

    for parity in (0, 1):

        @pl.when(jnp.logical_and(d == 0, odd == parity))
        def _(parity=parity):
            for n in range(4):
                group, m = names[2 * n + parity]
                for i in range(nb):
                    both = [r[2 * group + i % 2][m, turn[i] // 2] for r in (own_refs, other_refs)]
                    both = dot(jnp.concatenate(both, axis=1), keep[...]).astype(BF)
                    place(4 * kt, lax.rem(zh + n + parity * zl, 4), i, both)

    value = dot(left[...], right[...]).astype(BF)
    for to, out in enumerate(outs):

        @pl.when(d == to)
        def _(out=out):
            out[0] = value


def product(scalars, left, keep, slabs, owns, others, turn):
    _, nb, kt, t = slabs[0].shape
    rows, depth = left.shape[0] // 4, left.shape[1]
    names = {g: (at, m) for at, group in enumerate(GROUPS) for m, g in enumerate(group)}
    arrays = [slabs[0], slabs[2], slabs[6], *slabs[4], *owns, *others]
    return pl.pallas_call(
        functools.partial(product_kernel, turn, names),
        out_shape=[jax.ShapeDtypeStruct((2, rows, nb * t), BF)] * 4,
        grid_spec=pltpu.PrefetchScalarGridSpec(
            num_scalar_prefetch=1,
            grid=(2, 4),
            in_specs=[
                pl.BlockSpec((rows, depth), lambda o, d, _: (d, 0)),
                whole(keep.shape),
                *[whole(a.shape) for a in arrays],
            ],
            out_specs=[pl.BlockSpec((1, rows, nb * t), lambda o, d, _: (o, 0, 0))] * 4,
            scratch_shapes=[pltpu.VMEM((depth, nb * t), BF)],
        ),
        cost_estimate=pl.CostEstimate(
            flops=2 * 8 * rows * depth * nb * t,
            bytes_accessed=2 * left.size + 2 * nb * kt * t * 24,
            transcendentals=0,
        ),
        compiler_params=pltpu.CompilerParams(dimension_semantics=("arbitrary", "arbitrary")),
    )(scalars, left, keep, *arrays)


def arrange_kernel(count, adds, scalar, *refs):
    tables, pieces, out = refs[:count], refs[count : 2 * count], refs[-1]
    zl = scalar[0]
    u = tables[0].shape[1] // 256
    wide = out.shape[1] // u
    z = []
    for half in (0, 1):
        z.append(sum(dot(p[zl ^ half], table[...]) for p, table in zip(pieces, tables)))
    for r in range(u):
        low = z[0][:, r * 256 : (r + 1) * 256]
        high = pltpu.roll(z[1][:, r * 256 : (r + 1) * 256], 64, 1)
        for n, v in enumerate((low[:, :128], low[:, 128:] + high[:, :128], high[:, 128:])):
            at = slice(r * wide + n * 128, r * wide + (n + 1) * 128)
            v = v.astype(BF)
            out[:, at] = v + refs[2 * count][:, at] if adds else v


def arrange(scalars, gather, pieces, given, va, vb, before):
    rows, k = pieces[0].shape[1], gather.shape[0] // 4
    block = pl.BlockSpec((rows, va // 3 * vb), lambda s, _: (0, s))
    adds = before is not None

    def table(d):
        return pl.BlockSpec((k, gather.shape[1]), lambda s, _: (lax.rem(d + 2 * lax.rem(s, 2), 4), 0))

    return pl.pallas_call(
        functools.partial(arrange_kernel, len(given), adds),
        out_shape=jax.ShapeDtypeStruct((rows, va * vb), BF),
        grid_spec=pltpu.PrefetchScalarGridSpec(
            num_scalar_prefetch=1,
            grid=(3,),
            in_specs=[table(d) for d in given]
            + [pl.BlockSpec((2, rows, k), lambda s, _: (0, 0, s)) for _ in given]
            + [block] * adds,
            out_specs=block,
        ),
        input_output_aliases={1 + 2 * len(given): 0} if adds else {},
        cost_estimate=pl.CostEstimate(
            flops=12 * rows * gather.shape[1] * k * len(given),
            bytes_accessed=2 * rows * va * vb,
            transcendentals=0,
        ),
        compiler_params=pltpu.CompilerParams(dimension_semantics=("arbitrary",)),
    )(scalars, *[gather] * len(given), *pieces, *([before] if adds else []))


def left_kernel(oi, scalar, own, other, out):
    rows, depth = own.shape[1] // 2, own.shape[2]
    run = 4 * oi
    for n, given in enumerate((own, other)):
        direct = slice(n * depth, (n + 1) * depth)
        turned = slice((2 + n) * depth, (3 + n) * depth)
        for d in range(4):
            xi = lax.rem(scalar[3] + d, 4)
            out[d * rows : (d + 1) * rows, direct] = given[xi, :rows, :]
            for i in range(oi):
                at = pl.ds(pl.multiple_of(rows + (xi * oi + i) * run, run), run)
                blocks = [given[xj, at, :].astype(F32) for xj in range(4)]
                order = [blocks[xj][z * oi : (z + 1) * oi] for z in range(4) for xj in range(4)]
                to = d * rows + i * 4 * run
                out[to : to + 4 * run, turned] = jnp.concatenate(order, axis=0).astype(BF)


def amplitude_columns(amplitudes):
    oi, oj, kk = amplitudes.shape
    rows = oi * oj
    direct = jnp.transpose(amplitudes, (2, 0, 1)).reshape(kk, rows)
    turned = amplitudes.reshape(oi, 4, 4 * oi, kk)
    turned = lax.all_to_all(jnp.transpose(turned, (1, 3, 0, 2)), "zh", 0, 0, tiled=True)
    turned = jnp.transpose(turned, (1, 3, 0, 2)).reshape(kk, rows)
    amp = jnp.concatenate([direct, turned], axis=1)
    return jnp.broadcast_to(amp[None], (8, kk, 2 * rows))


def amplitude_rows(scalars, amp, oi):
    amp = lax.all_to_all(amp, ("zl", "y"), 0, 0, tiled=True)
    both = amp.shape[2]
    amp = jnp.transpose(amp.reshape(-1, both))
    amp = jnp.broadcast_to(amp[None], (4, *amp.shape))
    amp = lax.all_to_all(amp, "x", 0, 0, tiled=True)
    other = send(amp, along("core", 1))
    shape = (2 * both, 4 * amp.shape[2])
    return pl.pallas_call(
        functools.partial(left_kernel, oi),
        out_shape=jax.ShapeDtypeStruct(shape, BF),
        grid_spec=pltpu.PrefetchScalarGridSpec(
            num_scalar_prefetch=1,
            grid=(1,),
            in_specs=[whole(amp.shape)] * 2,
            out_specs=whole(shape),
        ),
        cost_estimate=pl.CostEstimate(flops=0, bytes_accessed=16 * both * amp.shape[2], transcendentals=0),
    )(scalars, amp, other)


def per_device(amplitudes, integrals):
    oi, oj, kk = amplitudes.shape
    va, vb = integrals.shape[1:]
    u = va // 3
    t = 2 * u * u
    zh, x, zl, y, core = (lax.axis_index(a) for a in AXES)
    scalars = jnp.stack([zl, zh, core, x])

    dx, s2, a8, cb, b8 = digits((4, 3, u, 2, u))
    yb = (dx - y - 2 * (s2 % 2)) % 4
    source = (((a8 * 4 + yb) * 2 + cb) * 3 + s2) * u + b8
    spread = one_hot(source, 12 * t)
    v = integrals.reshape(kk, 3, u, 2, vb // 2)
    v = jnp.transpose(v, (3, 1, 0, 2, 4)).reshape(6 * kk, u * vb // 2)
    v = dot(v, spread).astype(BF)
    v = v.reshape(2, 3, kk, 4, 3, t)
    v = jnp.stack([v[:, 0], jnp.roll(v[:, 1], 2, axis=2), v[:, 2]], axis=1)
    v = jnp.transpose(v, (3, 0, 1, 4, 2, 5))
    amp = amplitude_columns(amplitudes)
    v, amp = lax.optimization_barrier((v, amp))
    v = lax.all_to_all(v.reshape(4, -1, t), "x", 0, 0, tiled=True)
    left = amplitude_rows(scalars, amp, oi)
    v = v.reshape(4, 2, 3, 3, kk, t)

    a8, cb, b8 = digits((u, 2, u))
    place = (b8 * 2 + core) * u + a8
    keep = one_hot(jnp.where(cb == core, place, t + place), 2 * t)

    a8, lane = digits((u, 256))
    yb, rest = lane // (6 * u), lane % (6 * u)
    cb, s2, b8 = rest // (3 * u), rest // u % 3, rest % u
    dd = (x - y - yb - 2 * (s2 % 2)) % 4
    source = (((dd * 3 + s2) * u + a8) * 2 + cb) * u + b8
    gather = one_hot(jnp.where(lane < 24 * u, source, -1), 12 * t)

    slab = jnp.transpose(v.reshape(2, 2, 2, 9, kk, t), (2, 3, 1, 0, 4, 5)).reshape(2, 9, 4 * kk, t)
    slabs = {0: slab}
    up = down = slab
    owns, others = [], []

    def reflect(group):
        part = [
            jnp.where(zl == 0, *slabs[g]) if g == 4 else lax.dynamic_index_in_dim(slabs[g], zl, 0, False)
            for g in group
        ]
        part = jnp.stack(part)
        for odd in (0, 1):
            owns.append(send(part[:, odd::2], mirror(odd)))
        for own in owns[-2:]:
            others.append(send(own, along("core", 1)))

    for step, group in zip((1, 2, 3), GROUPS):
        up, down = send(up, along_z(1)), send(down, along_z(-1))
        reflect(group)
        slabs[8 - step], slabs[step] = up, down
        up, down, _ = lax.optimization_barrier((up, down, owns[-2:]))
    slabs[4] = (send(up[0], along_z(1)), send(down[1], along_z(-1)))
    for group in GROUPS[3:]:
        reflect(group)
    turn = [TILES.index((q, s)) for s, q in TILES]
    outs = product(scalars, left, keep, slabs, owns, others, turn)
    away = {d: send(outs[d], along("x", d)) for d in (1, 3, 2)}
    final = arrange(scalars, gather, [outs[0], away[1], away[3]], (0, 1, 3), va, vb, None)
    final = arrange(scalars, gather, [away[2]], (2,), va, vb, final)
    return final.reshape(oi, oj, va, vb)


def solution(mesh):
    fine = Mesh(mesh.devices.reshape(SIZES), AXES)
    row, col = ("zh", "x"), ("zl", "y", "core")
    return jax.shard_map(
        per_device,
        mesh=fine,
        in_specs=(P(row, None, col), P(row, col, None)),
        out_specs=P(row, None, col, None),
        check_vma=False,
    )
```

```python
import functools

import jax
import jax.numpy as jnp
import numpy as np
from jax import lax
from jax.experimental import pallas as pl
from jax.experimental.pallas import tpu as pltpu
from jax.sharding import Mesh, PartitionSpec as P

AXES = ("zh", "x", "zl", "y", "core")
SIZES = (4, 4, 2, 4, 2)
BF = jnp.bfloat16
F32 = jnp.float32
TILES = tuple((s, q) for s in range(3) for q in range(3))
GROUPS = ((0,), (1, 7), (2, 6), (3, 5), (4,))


def pairs(move):
    out = []
    for i in range(256):
        here = dict(zip(AXES, (int(v) for v in np.unravel_index(i, SIZES))))
        there = move(dict(here))
        out.append((i, int(np.ravel_multi_index([there[a] for a in AXES], SIZES))))
    return out


def along_z(step):
    def move(d):
        z = (d["zh"] * 2 + d["zl"] + step) % 8
        d["zh"], d["zl"] = z // 2, z % 2
        return d

    return pairs(move)


def along(axis, step):
    size = SIZES[AXES.index(axis)]

    def move(d):
        d[axis] = (d[axis] + step) % size
        return d

    return pairs(move)


def mirror(odd):
    def move(d):
        d["y"] = (d["x"] - d["y"] - 2 * odd) % 4
        return d

    return pairs(move)


def send(value, table):
    return lax.ppermute(value, AXES, table)


def one_hot(source, rows):
    at = lax.broadcasted_iota(jnp.int32, (rows, source.shape[0]), 0)
    return (at == source[None, :]).astype(BF)


def digits(sizes):
    n = int(np.prod(sizes))
    return [jnp.asarray(v, jnp.int32) for v in np.unravel_index(np.arange(n), sizes)]


def dot(a, b):
    return jnp.dot(a, b, preferred_element_type=F32)


def whole(shape):
    zeros = (0,) * len(shape)
    return pl.BlockSpec(shape, lambda *_: zeros, pipeline_mode=pl.Buffered(1))


def product_kernel(turn, names, scalar, left, keep, *refs):
    slabs = {g: r for g, r in zip((0, 2, 6), refs[:3])}
    four = refs[3:5]
    n_groups = 2 * len(GROUPS)
    own_refs, other_refs = refs[5 : 5 + n_groups], refs[5 + n_groups : 5 + 2 * n_groups]
    outs, right = refs[-5:-1], refs[-1]
    odd, d = pl.program_id(0), pl.program_id(1)
    zl, zh, core = scalar[0], scalar[1], scalar[2]
    nb, kt, t = slabs[0].shape[1:]
    half, part = zl ^ odd, kt // 2

    def place(base, at, i, value):
        for c in (0, 1):
            to = base + (c ^ core) * (4 * part) + at * part
            to = pl.ds(pl.multiple_of(to, part), part)
            right[to, i * t : (i + 1) * t] = value[c * part : (c + 1) * part]

    @pl.when(d == 0)
    def _():
        for n, g in enumerate((0, 2, 4, 6)):
            for i in range(nb):
                if g == 4:
                    v = jnp.where(half == 0, four[0][i], four[1][i])
                else:
                    v = slabs[g][half, i]
                place(0, lax.rem(zh + n, 4), i, v)

    for parity in (0, 1):

        @pl.when(jnp.logical_and(d == 0, odd == parity))
        def _(parity=parity):
            for n in range(4):
                group, m = names[2 * n + parity]
                for i in range(nb):
                    both = [r[2 * group + i % 2][m, turn[i] // 2] for r in (own_refs, other_refs)]
                    both = dot(jnp.concatenate(both, axis=1), keep[...]).astype(BF)
                    place(4 * kt, lax.rem(zh + n + parity * zl, 4), i, both)

    value = dot(left[...], right[...]).astype(BF)
    for to, out in enumerate(outs):

        @pl.when(d == to)
        def _(out=out):
            out[0] = value


def product(scalars, left, keep, slabs, owns, others, turn):
    _, nb, kt, t = slabs[0].shape
    rows, depth = left.shape[0] // 4, left.shape[1]
    names = {g: (at, m) for at, group in enumerate(GROUPS) for m, g in enumerate(group)}
    arrays = [slabs[0], slabs[2], slabs[6], *slabs[4], *owns, *others]
    return pl.pallas_call(
        functools.partial(product_kernel, turn, names),
        out_shape=[jax.ShapeDtypeStruct((2, rows, nb * t), BF)] * 4,
        grid_spec=pltpu.PrefetchScalarGridSpec(
            num_scalar_prefetch=1,
            grid=(2, 4),
            in_specs=[
                pl.BlockSpec((rows, depth), lambda o, d, _: (d, 0)),
                whole(keep.shape),
                *[whole(a.shape) for a in arrays],
            ],
            out_specs=[pl.BlockSpec((1, rows, nb * t), lambda o, d, _: (o, 0, 0))] * 4,
            scratch_shapes=[pltpu.VMEM((depth, nb * t), BF)],
        ),
        cost_estimate=pl.CostEstimate(
            flops=2 * 8 * rows * depth * nb * t,
            bytes_accessed=2 * left.size + 2 * nb * kt * t * 24,
            transcendentals=0,
        ),
        compiler_params=pltpu.CompilerParams(dimension_semantics=("arbitrary", "arbitrary")),
    )(scalars, left, keep, *arrays)


def arrange_kernel(count, adds, scalar, *refs):
    tables, pieces, out = refs[:count], refs[count : 2 * count], refs[-1]
    zl = scalar[0]
    u = tables[0].shape[1] // 256
    wide = out.shape[1] // u
    z = []
    for half in (0, 1):
        z.append(sum(dot(p[zl ^ half], table[...]) for p, table in zip(pieces, tables)))
    for r in range(u):
        low = z[0][:, r * 256 : (r + 1) * 256]
        high = pltpu.roll(z[1][:, r * 256 : (r + 1) * 256], 64, 1)
        for n, v in enumerate((low[:, :128], low[:, 128:] + high[:, :128], high[:, 128:])):
            at = slice(r * wide + n * 128, r * wide + (n + 1) * 128)
            v = v.astype(BF)
            out[:, at] = v + refs[2 * count][:, at] if adds else v


def arrange(scalars, gather, pieces, given, va, vb, before):
    rows, k = pieces[0].shape[1], gather.shape[0] // 4
    block = pl.BlockSpec((rows, va // 3 * vb), lambda s, _: (0, s))
    adds = before is not None

    def table(d):
        return pl.BlockSpec((k, gather.shape[1]), lambda s, _: (lax.rem(d + 2 * lax.rem(s, 2), 4), 0))

    return pl.pallas_call(
        functools.partial(arrange_kernel, len(given), adds),
        out_shape=jax.ShapeDtypeStruct((rows, va * vb), BF),
        grid_spec=pltpu.PrefetchScalarGridSpec(
            num_scalar_prefetch=1,
            grid=(3,),
            in_specs=[table(d) for d in given]
            + [pl.BlockSpec((2, rows, k), lambda s, _: (0, 0, s)) for _ in given]
            + [block] * adds,
            out_specs=block,
        ),
        input_output_aliases={1 + 2 * len(given): 0} if adds else {},
        cost_estimate=pl.CostEstimate(
            flops=12 * rows * gather.shape[1] * k * len(given),
            bytes_accessed=2 * rows * va * vb,
            transcendentals=0,
        ),
        compiler_params=pltpu.CompilerParams(dimension_semantics=("arbitrary",)),
    )(scalars, *[gather] * len(given), *pieces, *([before] if adds else []))


def left_kernel(oi, scalar, own, other, out):
    rows, depth = own.shape[1] // 2, own.shape[2]
    run = 4 * oi
    for n, given in enumerate((own, other)):
        direct = slice(n * depth, (n + 1) * depth)
        turned = slice((2 + n) * depth, (3 + n) * depth)
        for d in range(4):
            xi = lax.rem(scalar[3] + d, 4)
            out[d * rows : (d + 1) * rows, direct] = given[xi, :rows, :]
            for i in range(oi):
                at = pl.ds(pl.multiple_of(rows + (xi * oi + i) * run, run), run)
                blocks = [given[xj, at, :].astype(F32) for xj in range(4)]
                order = [blocks[xj][z * oi : (z + 1) * oi] for z in range(4) for xj in range(4)]
                to = d * rows + i * 4 * run
                out[to : to + 4 * run, turned] = jnp.concatenate(order, axis=0).astype(BF)


def amplitude_columns(amplitudes):
    oi, oj, kk = amplitudes.shape
    rows = oi * oj
    direct = jnp.transpose(amplitudes, (2, 0, 1)).reshape(kk, rows)
    turned = amplitudes.reshape(oi, 4, 4 * oi, kk)
    turned = lax.all_to_all(jnp.transpose(turned, (1, 3, 0, 2)), "zh", 0, 0, tiled=True)
    turned = jnp.transpose(turned, (1, 3, 0, 2)).reshape(kk, rows)
    amp = jnp.concatenate([direct, turned], axis=1)
    return jnp.broadcast_to(amp[None], (8, kk, 2 * rows))


def amplitude_rows(scalars, amp, oi):
    amp = lax.all_to_all(amp, ("zl", "y"), 0, 0, tiled=True)
    both = amp.shape[2]
    amp = jnp.transpose(amp.reshape(-1, both))
    amp = jnp.broadcast_to(amp[None], (4, *amp.shape))
    amp = lax.all_to_all(amp, "x", 0, 0, tiled=True)
    other = send(amp, along("core", 1))
    shape = (2 * both, 4 * amp.shape[2])
    return pl.pallas_call(
        functools.partial(left_kernel, oi),
        out_shape=jax.ShapeDtypeStruct(shape, BF),
        grid_spec=pltpu.PrefetchScalarGridSpec(
            num_scalar_prefetch=1,
            grid=(1,),
            in_specs=[whole(amp.shape)] * 2,
            out_specs=whole(shape),
        ),
        cost_estimate=pl.CostEstimate(flops=0, bytes_accessed=16 * both * amp.shape[2], transcendentals=0),
    )(scalars, amp, other)


def per_device(amplitudes, integrals):
    oi, oj, kk = amplitudes.shape
    va, vb = integrals.shape[1:]
    u = va // 3
    t = 2 * u * u
    zh, x, zl, y, core = (lax.axis_index(a) for a in AXES)
    scalars = jnp.stack([zl, zh, core, x])

    dx, s2, a8, cb, b8 = digits((4, 3, u, 2, u))
    yb = (dx - y - 2 * (s2 % 2)) % 4
    source = (((a8 * 4 + yb) * 2 + cb) * 3 + s2) * u + b8
    spread = one_hot(source, 12 * t)
    v = integrals.reshape(kk, 3, u, 2, vb // 2)
    v = jnp.transpose(v, (3, 1, 0, 2, 4)).reshape(6 * kk, u * vb // 2)
    v = dot(v, spread).astype(BF)
    v = v.reshape(2, 3, kk, 4, 3, t)
    v = jnp.stack([v[:, 0], jnp.roll(v[:, 1], 2, axis=2), v[:, 2]], axis=1)
    v = jnp.transpose(v, (3, 0, 1, 4, 2, 5))
    amp = amplitude_columns(amplitudes)
    v, amp = lax.optimization_barrier((v, amp))
    v = lax.all_to_all(v.reshape(4, -1, t), "x", 0, 0, tiled=True)
    left = amplitude_rows(scalars, amp, oi)
    v = v.reshape(4, 2, 3, 3, kk, t)

    a8, cb, b8 = digits((u, 2, u))
    place = (b8 * 2 + core) * u + a8
    keep = one_hot(jnp.where(cb == core, place, t + place), 2 * t)

    a8, lane = digits((u, 256))
    yb, rest = lane // (6 * u), lane % (6 * u)
    cb, s2, b8 = rest // (3 * u), rest // u % 3, rest % u
    dd = (x - y - yb - 2 * (s2 % 2)) % 4
    source = (((dd * 3 + s2) * u + a8) * 2 + cb) * u + b8
    gather = one_hot(jnp.where(lane < 24 * u, source, -1), 12 * t)

    slab = jnp.transpose(v.reshape(2, 2, 2, 9, kk, t), (2, 3, 1, 0, 4, 5)).reshape(2, 9, 4 * kk, t)
    slabs = {0: slab}
    up = down = slab
    owns, others = [], []

    def reflect(group):
        part = [
            jnp.where(zl == 0, *slabs[g]) if g == 4 else lax.dynamic_index_in_dim(slabs[g], zl, 0, False)
            for g in group
        ]
        part = jnp.stack(part)
        if group == (4,):
            part, _ = lax.optimization_barrier((part, left))
        for odd in (0, 1):
            owns.append(send(part[:, odd::2], mirror(odd)))
        for own in owns[-2:]:
            others.append(send(own, along("core", 1)))

    for step, group in zip((1, 2, 3), GROUPS):
        up, down = send(up, along_z(1)), send(down, along_z(-1))
        reflect(group)
        slabs[8 - step], slabs[step] = up, down
        up, down, _ = lax.optimization_barrier((up, down, owns[-2:]))
    slabs[4] = (send(up[0], along_z(1)), send(down[1], along_z(-1)))
    for group in GROUPS[3:]:
        reflect(group)
    turn = [TILES.index((q, s)) for s, q in TILES]
    outs = product(scalars, left, keep, slabs, owns, others, turn)
    away = {d: send(outs[d], along("x", d)) for d in (1, 3)}
    far, near, gather = lax.optimization_barrier((outs[2], away, gather))
    away = {**near, 2: send(far, along("x", 2))}
    final = arrange(scalars, gather, [outs[0], away[1], away[3]], (0, 1, 3), va, vb, None)
    final = arrange(scalars, gather, [away[2]], (2,), va, vb, final)
    return final.reshape(oi, oj, va, vb)


def solution(mesh):
    fine = Mesh(mesh.devices.reshape(SIZES), AXES)
    row, col = ("zh", "x"), ("zl", "y", "core")
    return jax.shard_map(
        per_device,
        mesh=fine,
        in_specs=(P(row, None, col), P(row, col, None)),
        out_specs=P(row, None, col, None),
        check_vma=False,
    )
```

```python
import functools

import jax
import jax.numpy as jnp
import numpy as np
from jax import lax
from jax.experimental import pallas as pl
from jax.experimental.pallas import tpu as pltpu
from jax.sharding import Mesh, PartitionSpec as P

AXES = ("zh", "x", "zl", "y", "core")
SIZES = (4, 4, 2, 4, 2)
BF = jnp.bfloat16
F32 = jnp.float32
TILES = tuple((s, q) for s in range(3) for q in range(3))
GROUPS = ((0,), (1, 7), (2, 6), (3, 5), (4,))


def pairs(move):
    out = []
    for i in range(256):
        here = dict(zip(AXES, (int(v) for v in np.unravel_index(i, SIZES))))
        there = move(dict(here))
        out.append((i, int(np.ravel_multi_index([there[a] for a in AXES], SIZES))))
    return out


def along_z(step):
    def move(d):
        z = (d["zh"] * 2 + d["zl"] + step) % 8
        d["zh"], d["zl"] = z // 2, z % 2
        return d

    return pairs(move)


def along(axis, step):
    size = SIZES[AXES.index(axis)]

    def move(d):
        d[axis] = (d[axis] + step) % size
        return d

    return pairs(move)


def mirror(odd):
    def move(d):
        d["y"] = (d["x"] - d["y"] - 2 * odd) % 4
        return d

    return pairs(move)


def send(value, table):
    return lax.ppermute(value, AXES, table)


def one_hot(source, rows):
    at = lax.broadcasted_iota(jnp.int32, (rows, source.shape[0]), 0)
    return (at == source[None, :]).astype(BF)


def digits(sizes):
    n = int(np.prod(sizes))
    return [jnp.asarray(v, jnp.int32) for v in np.unravel_index(np.arange(n), sizes)]


def dot(a, b):
    return jnp.dot(a, b, preferred_element_type=F32)


def whole(shape):
    zeros = (0,) * len(shape)
    return pl.BlockSpec(shape, lambda *_: zeros, pipeline_mode=pl.Buffered(1))


def product_kernel(turn, names, odd, scalar, left, keep, *refs):
    slabs = {g: r for g, r in zip((0, 2, 6), refs[:3])}
    four = refs[3:5]
    n_groups = (len(refs) - 10) // 2
    own_refs, other_refs = refs[5 : 5 + n_groups], refs[5 + n_groups : 5 + 2 * n_groups]
    outs, right = refs[-5:-1], refs[-1]
    d = pl.program_id(0)
    zl, zh, core = scalar[0], scalar[1], scalar[2]
    nb, kt, t = slabs[0].shape[1:]
    half, part = zl ^ odd, kt // 2

    def place(base, at, i, value):
        for c in (0, 1):
            to = base + (c ^ core) * (4 * part) + at * part
            to = pl.ds(pl.multiple_of(to, part), part)
            right[to, i * t : (i + 1) * t] = value[c * part : (c + 1) * part]

    @pl.when(d == 0)
    def _():
        for n, g in enumerate((0, 2, 4, 6)):
            for i in range(nb):
                if g == 4:
                    v = jnp.where(half == 0, four[0][i], four[1][i])
                else:
                    v = slabs[g][half, i]
                place(0, lax.rem(zh + n, 4), i, v)

        for n in range(4):
            group, m = names[2 * n + odd]
            for i in range(nb):
                both = [r[2 * group + i % 2][m, turn[i] // 2] for r in (own_refs, other_refs)]
                both = dot(jnp.concatenate(both, axis=1), keep[...]).astype(BF)
                place(4 * kt, lax.rem(zh + n + odd * zl, 4), i, both)

    value = dot(left[...], right[...]).astype(BF)
    for to, out in enumerate(outs):

        @pl.when(d == to)
        def _(out=out):
            out[...] = value


def product(scalars, left, keep, slabs, owns, others, turn, odd):
    _, nb, kt, t = slabs[0].shape
    rows, depth = left.shape[0] // 4, left.shape[1]
    need = [n for n, group in enumerate(GROUPS) if group[0] % 2 == odd]
    names = {g: (at, m) for at, n in enumerate(need) for m, g in enumerate(GROUPS[n])}
    owns, others = ([v[2 * n + h] for n in need for h in (0, 1)] for v in (owns, others))
    arrays = [slabs[0], slabs[2], slabs[6], *slabs[4], *owns, *others]
    return pl.pallas_call(
        functools.partial(product_kernel, turn, names, odd),
        out_shape=[jax.ShapeDtypeStruct((rows, nb * t), BF)] * 4,
        grid_spec=pltpu.PrefetchScalarGridSpec(
            num_scalar_prefetch=1,
            grid=(4,),
            in_specs=[
                pl.BlockSpec((rows, depth), lambda d, _: (d, 0)),
                whole(keep.shape),
                *[whole(a.shape) for a in arrays],
            ],
            out_specs=[whole((rows, nb * t))] * 4,
            scratch_shapes=[pltpu.VMEM((depth, nb * t), BF)],
        ),
        cost_estimate=pl.CostEstimate(
            flops=2 * 4 * rows * depth * nb * t,
            bytes_accessed=2 * left.size + 2 * nb * kt * t * 12,
            transcendentals=0,
        ),
        compiler_params=pltpu.CompilerParams(dimension_semantics=("arbitrary",)),
    )(scalars, left, keep, *arrays)


def arrange_kernel(count, adds, scalar, *refs):
    tables, even, odd, out = refs[:count], refs[count : 2 * count], refs[2 * count : 3 * count], refs[-1]
    zl = scalar[0]
    u = tables[0].shape[1] // 256
    wide = out.shape[1] // u
    z = []
    for half in (0, 1):
        pieces = [jnp.where(zl == half, p[...], q[...]) for p, q in zip(even, odd)]
        z.append(sum(dot(p, table[...]) for p, table in zip(pieces, tables)))
    for r in range(u):
        low = z[0][:, r * 256 : (r + 1) * 256]
        high = pltpu.roll(z[1][:, r * 256 : (r + 1) * 256], 64, 1)
        for n, v in enumerate((low[:, :128], low[:, 128:] + high[:, :128], high[:, 128:])):
            at = slice(r * wide + n * 128, r * wide + (n + 1) * 128)
            v = v.astype(BF)
            out[:, at] = v + refs[3 * count][:, at] if adds else v


def arrange(scalars, gather, pieces, given, va, vb, before):
    rows, k = pieces[0].shape[0], gather.shape[0] // 4
    block = pl.BlockSpec((rows, va // 3 * vb), lambda s, _: (0, s))
    adds = before is not None

    def table(d):
        return pl.BlockSpec((k, gather.shape[1]), lambda s, _: (lax.rem(d + 2 * lax.rem(s, 2), 4), 0))

    return pl.pallas_call(
        functools.partial(arrange_kernel, len(given), adds),
        out_shape=jax.ShapeDtypeStruct((rows, va * vb), BF),
        grid_spec=pltpu.PrefetchScalarGridSpec(
            num_scalar_prefetch=1,
            grid=(3,),
            in_specs=[table(d) for d in given]
            + [pl.BlockSpec((rows, k), lambda s, _: (0, s))] * (2 * len(given))
            + [block] * adds,
            out_specs=block,
        ),
        input_output_aliases={1 + 3 * len(given): 0} if adds else {},
        cost_estimate=pl.CostEstimate(
            flops=12 * rows * gather.shape[1] * k * len(given),
            bytes_accessed=2 * rows * va * vb,
            transcendentals=0,
        ),
        compiler_params=pltpu.CompilerParams(dimension_semantics=("arbitrary",)),
    )(scalars, *[gather] * len(given), *pieces, *([before] if adds else []))


def left_kernel(oi, scalar, own, other, out):
    rows, depth = own.shape[1] // 2, own.shape[2]
    run = 4 * oi
    for n, given in enumerate((own, other)):
        direct = slice(n * depth, (n + 1) * depth)
        turned = slice((2 + n) * depth, (3 + n) * depth)
        for d in range(4):
            xi = lax.rem(scalar[3] + d, 4)
            out[d * rows : (d + 1) * rows, direct] = given[xi, :rows, :]
            for i in range(oi):
                at = pl.ds(pl.multiple_of(rows + (xi * oi + i) * run, run), run)
                blocks = [given[xj, at, :].astype(F32) for xj in range(4)]
                order = [blocks[xj][z * oi : (z + 1) * oi] for z in range(4) for xj in range(4)]
                to = d * rows + i * 4 * run
                out[to : to + 4 * run, turned] = jnp.concatenate(order, axis=0).astype(BF)


def amplitude_columns(amplitudes):
    oi, oj, kk = amplitudes.shape
    rows = oi * oj
    direct = jnp.transpose(amplitudes, (2, 0, 1)).reshape(kk, rows)
    turned = amplitudes.reshape(oi, 4, 4 * oi, kk)
    turned = lax.all_to_all(jnp.transpose(turned, (1, 3, 0, 2)), "zh", 0, 0, tiled=True)
    turned = jnp.transpose(turned, (1, 3, 0, 2)).reshape(kk, rows)
    amp = jnp.concatenate([direct, turned], axis=1)
    return jnp.broadcast_to(amp[None], (8, kk, 2 * rows))


def amplitude_rows(scalars, amp, oi):
    amp = lax.all_to_all(amp, ("zl", "y"), 0, 0, tiled=True)
    both = amp.shape[2]
    amp = jnp.transpose(amp.reshape(-1, both))
    amp = jnp.broadcast_to(amp[None], (4, *amp.shape))
    amp = lax.all_to_all(amp, "x", 0, 0, tiled=True)
    other = send(amp, along("core", 1))
    shape = (2 * both, 4 * amp.shape[2])
    return pl.pallas_call(
        functools.partial(left_kernel, oi),
        out_shape=jax.ShapeDtypeStruct(shape, BF),
        grid_spec=pltpu.PrefetchScalarGridSpec(
            num_scalar_prefetch=1,
            grid=(1,),
            in_specs=[whole(amp.shape)] * 2,
            out_specs=whole(shape),
        ),
        cost_estimate=pl.CostEstimate(flops=0, bytes_accessed=16 * both * amp.shape[2], transcendentals=0),
    )(scalars, amp, other)


def per_device(amplitudes, integrals):
    oi, oj, kk = amplitudes.shape
    va, vb = integrals.shape[1:]
    u = va // 3
    t = 2 * u * u
    zh, x, zl, y, core = (lax.axis_index(a) for a in AXES)
    scalars = jnp.stack([zl, zh, core, x])

    dx, s2, a8, cb, b8 = digits((4, 3, u, 2, u))
    yb = (dx - y - 2 * (s2 % 2)) % 4
    source = (((a8 * 4 + yb) * 2 + cb) * 3 + s2) * u + b8
    spread = one_hot(source, 12 * t)
    v = integrals.reshape(kk, 3, u, 2, vb // 2)
    v = jnp.transpose(v, (3, 1, 0, 2, 4)).reshape(6 * kk, u * vb // 2)
    v = dot(v, spread).astype(BF)
    v = v.reshape(2, 3, kk, 4, 3, t)
    v = jnp.stack([v[:, 0], jnp.roll(v[:, 1], 2, axis=2), v[:, 2]], axis=1)
    v = jnp.transpose(v, (3, 0, 1, 4, 2, 5))
    amp = amplitude_columns(amplitudes)
    v, amp = lax.optimization_barrier((v, amp))
    v = lax.all_to_all(v.reshape(4, -1, t), "x", 0, 0, tiled=True)
    left = amplitude_rows(scalars, amp, oi)
    v = v.reshape(4, 2, 3, 3, kk, t)

    a8, cb, b8 = digits((u, 2, u))
    place = (b8 * 2 + core) * u + a8
    keep = one_hot(jnp.where(cb == core, place, t + place), 2 * t)

    a8, lane = digits((u, 256))
    yb, rest = lane // (6 * u), lane % (6 * u)
    cb, s2, b8 = rest // (3 * u), rest // u % 3, rest % u
    dd = (x - y - yb - 2 * (s2 % 2)) % 4
    source = (((dd * 3 + s2) * u + a8) * 2 + cb) * u + b8
    gather = one_hot(jnp.where(lane < 24 * u, source, -1), 12 * t)

    slab = jnp.transpose(v.reshape(2, 2, 2, 9, kk, t), (2, 3, 1, 0, 4, 5)).reshape(2, 9, 4 * kk, t)
    slabs = {0: slab}
    up = down = slab
    owns, others = [], []

    def reflect(group):
        part = [
            jnp.where(zl == 0, *slabs[g]) if g == 4 else lax.dynamic_index_in_dim(slabs[g], zl, 0, False)
            for g in group
        ]
        part = jnp.stack(part)
        if group == (4,):
            part, _ = lax.optimization_barrier((part, left))
        for odd in (0, 1):
            owns.append(send(part[:, odd::2], mirror(odd)))
        for own in owns[-2:]:
            others.append(send(own, along("core", 1)))

    for step, group in zip((1, 2, 3), GROUPS):
        up, down = send(up, along_z(1)), send(down, along_z(-1))
        reflect(group)
        slabs[8 - step], slabs[step] = up, down
        up, down, _ = lax.optimization_barrier((up, down, owns[-2:]))
    slabs[4] = (send(up[0], along_z(1)), send(down[1], along_z(-1)))
    for group in GROUPS[3:]:
        reflect(group)
    turn = [TILES.index((q, s)) for s, q in TILES]
    late = product(scalars, left, keep, slabs, owns, others, turn, 1)
    near = {(d, 1): send(late[d], along("x", d)) for d in (1, 3)}
    left, _ = lax.optimization_barrier((left, late))
    outs = (product(scalars, left, keep, slabs, owns, others, turn, 0), late)
    near.update({(d, 0): send(outs[0][d], along("x", d)) for d in (1, 3)})
    far, near, gather = lax.optimization_barrier(([out[2] for out in outs], near, gather))
    far = [send(out, along("x", 2)) for out in far]
    given = [outs[n][0] if d == 0 else near[d, n] for n in (0, 1) for d in (0, 1, 3)]
    final = arrange(scalars, gather, given, (0, 1, 3), va, vb, None)
    final = arrange(scalars, gather, far, (2,), va, vb, final)
    return final.reshape(oi, oj, va, vb)


def solution(mesh):
    fine = Mesh(mesh.devices.reshape(SIZES), AXES)
    row, col = ("zh", "x"), ("zl", "y", "core")
    return jax.shard_map(
        per_device,
        mesh=fine,
        in_specs=(P(row, None, col), P(row, col, None)),
        out_specs=P(row, None, col, None),
        check_vma=False,
    )
```
